32 devices in a mesh: tensor: 4 (over z), frames: 2 (over core), batch: 4 (over y, x).
Axes of the slice: x: 2, y: 2, z: 4, core: 2. Of those that a mesh axis runs over, the one named last changes fastest.
Arguments:
- tokens: bfloat16 [4, 2, 1024, 1024], P('batch', 'frames', 'tensor'), may hold values from -6 to 6
- cotangent: bfloat16 [4, 2, 1024, 1024], P('batch', 'frames', 'tensor'), may hold values from -6 to 6
- bucket: int32 [4], P('batch'), may hold values from 0 to 1, as said below
- clip_of_frame: int32 [4, 8], P('batch'), may hold values from 0 to 6, as said below
- noise_index: int32 [4, 8], P('batch'), may hold values from 0 to 999
- noise_table: float32 [1000, 1024], replicated, may hold values from -6 to 6
- w_mod: bfloat16 [1024, 6144], P(None, 'tensor'), may hold values from -0.1875 to 0.1875
- b_mod: bfloat16 [6144], P('tensor'), may hold values from -1.796875 to 1.796875
- w_qkv: bfloat16 [1024, 3, 1024], P(None, None, 'tensor'), may hold values from -0.1875 to 0.1875
- w_out: bfloat16 [1024, 1024], P('tensor'), may hold values from -1 to 1
- w_up: bfloat16 [1024, 4096], P(None, 'tensor'), may hold values from -0.1875 to 0.1875
- w_down: bfloat16 [4096, 1024], P('tensor'), may hold values from -0.09375 to 0.09375
Outputs:
- out: bfloat16 [4, 2, 1024, 1024], P('batch', 'frames', 'tensor')
- d_tokens: bfloat16 [4, 2, 1024, 1024], P('batch', 'frames', 'tensor')
- d_w_mod: float32 [1024, 6144], P(None, 'tensor')
- d_b_mod: float32 [6144], P('tensor')
- d_w_qkv: float32 [1024, 3, 1024], P(None, None, 'tensor')
- d_w_out: float32 [1024, 1024], P('tensor')
- d_w_up: float32 [1024, 4096], P(None, 'tensor')
- d_w_down: float32 [4096, 1024], P('tensor')
The draws below stay inside these ranges and needn't reach their ends.
Inputs may be any that keep to these rules, and one draw needn't show every extreme that they name: `bucket`: both values occur in every draw. `clip_of_frame`: A row starts at 0 and never falls; with F the row's frame count (2048 divided by its frame size), frames F // 2 - 1 and F // 2 share a clip; entries from frame F on repeat the clip of frame F - 1. In some pack of 16 by 16 patches every other frame starts a clip of its own. `noise_index`: only a row's first 2048 / (frame size) entries are read.
All inputs are finite; a program needn't handle non-finite values.
Results may differ from the reference program's by a relative error of at most 0.017.
The reference program's roundings to bfloat16 on the way count: a program that leaves them out, or rounds other values in their place, can miss the bound.
Values may be sent and summed in bfloat16 or wider, within the bound.
No kernel may reach another device: no remote copies, remote signals or barrier semaphores. Data moves between devices by JAX's collectives and lax.ppermute only.
A program may use at most 192 MiB of HBM per device.

```python
import jax
import jax.numpy as jnp
from jax import lax

D = 1024
HEADS = 16
HEAD_DIM = 64
FF = 4096
LEVELS = 1000
FRAME_SMALL = 256
FRAME_LARGE = 1024
SHARD_TOK = 1024
SEQ = 2048
MAXF = 8
BATCH = 4
N_FRAMES = 2


def pack_layout(key):
    grid_kind = jax.random.randint(jax.random.fold_in(key, 11), (BATCH,), 0, 2)
    grid_kind = grid_kind.at[0].set(1 - grid_kind[BATCH - 1])
    frame_total = jnp.where(grid_kind == 0, MAXF, MAXF * FRAME_SMALL // FRAME_LARGE)
    random_draw = jax.random.randint(jax.random.fold_in(key, 12), (BATCH, MAXF), 0, 4)
    frame_index = jnp.arange(MAXF)[None, :]
    full_row = jnp.where(grid_kind[0] == 0, 0, BATCH - 1)
    every_cut = jnp.arange(BATCH)[:, None] == full_row
    cut_here = ((random_draw == 0) | every_cut) & (frame_index > 0) & (frame_index < frame_total[:, None]) & (frame_index != frame_total[:, None] // 2)
    clip_ids = jnp.cumsum(cut_here.astype(jnp.int32), axis=1)
    return (grid_kind.astype(jnp.int32), clip_ids.astype(jnp.int32))


def draw_bucket(key, part):
    return pack_layout(key)[0]


def draw_clip_of_frame(key, part):
    return pack_layout(key)[1]


def set_ends(entries, stream_key, smallest, top_value):
    spot = [jax.random.randint(jax.random.fold_in(stream_key, axis), (), 0, length) for axis, length in enumerate(entries.shape)]
    main_axis = entries.shape.index(max(entries.shape))
    neighbour = spot[:main_axis] + [(spot[main_axis] + 1) % entries.shape[main_axis]] + spot[main_axis + 1:]
    return entries.at[tuple(spot)].set(smallest).at[tuple(neighbour)].set(top_value)


def levels(stream_key, extent, shards, least, top_value):
    gain, own = 1.0, jax.random.fold_in(stream_key, 6)
    for axis_at, parts in shards:
        draws = jnp.exp(jax.random.uniform(jax.random.fold_in(own, axis_at), (parts,), jnp.float32, least / len(shards), top_value / len(shards)))
        gain = gain * jnp.repeat(draws, extent[axis_at] // parts).reshape([-1 if axis == axis_at else 1 for axis in range(len(extent))])
    return gain


def noise(stream_key, shape, width, limit, shards=(), held_as=jnp.bfloat16):
    values = jax.random.normal(stream_key, shape, jnp.float32) * width
    if len(shards) > 0:
        values = levels(stream_key, shape, shards, -0.22, 0.18) * values
    return jnp.clip(values, min=-limit, max=limit).astype(held_as)


def setup_inputs(seed: int = 0) -> dict:
    key_list = jax.random.split(jax.random.key(seed), 13)
    return {
        "tokens": noise(key_list[0], (BATCH, N_FRAMES, SHARD_TOK, D), 1.0, 6.0, ((0, 4), (1, 2), (2, 4))),
        "cotangent": noise(key_list[1], (BATCH, N_FRAMES, SHARD_TOK, D), 1.0, 6.0, ((0, 4), (1, 2), (2, 4))),
        "bucket": draw_bucket(jax.random.fold_in(key_list[12], 71), 0),
        "clip_of_frame": draw_clip_of_frame(jax.random.fold_in(key_list[12], 71), 0),
        "noise_index": set_ends(jax.random.randint(key_list[4], (BATCH, MAXF), 0, LEVELS), jax.random.fold_in(key_list[4], 1), 0, LEVELS - 1).astype(jnp.int32),
        "noise_table": noise(key_list[5], (LEVELS, D), 1.0, 6.0, (), jnp.float32),
        "w_mod": noise(key_list[6], (D, 6 * D), D ** -0.5, 0.1875, ((1, 4),)),
        "b_mod": noise(key_list[7], (6 * D,), 0.3, 1.796875, ((0, 4),)),
        "w_qkv": noise(key_list[8], (D, 3, D), D ** -0.5, 0.1875, ((2, 4),)),
        "w_out": noise(key_list[9], (D, D), (D // 32) ** -0.5, 1.0, ((0, 4),)),
        "w_up": noise(key_list[10], (D, FF), D ** -0.5, 0.1875, ((1, 4),)),
        "w_down": noise(key_list[11], (FF, D), FF ** -0.5, 0.09375, ((0, 4),)),
    }


@jax.custom_vjp
def low(v):
    return lax.optimization_barrier(v.astype(jnp.bfloat16)).astype(jnp.float32)

@jax.custom_vjp
def low_back(v):
    return v

def low_keep(v):
    return (low(v), None)

def low_pass(kept, grad):
    return (grad,)

def back_keep(v):
    return (v, None)

def back_low(kept, grad):
    return (low(grad),)
low.defvjp(low_keep, low_pass)
low_back.defvjp(back_keep, back_low)
eps = 1e-06
highest = lax.Precision.HIGHEST

def normalized(values):
    centre = values - lax.optimization_barrier(jnp.mean(values, axis=-1, keepdims=True))
    spread = lax.optimization_barrier(jnp.mean(centre * centre, axis=-1, keepdims=True))
    return centre * lax.rsqrt(spread + eps)

def rotary(positions):
    half_dim = HEAD_DIM // 2
    frequency = 10000.0 ** (-(jnp.arange(half_dim, dtype=jnp.float32) * 2.0 / HEAD_DIM))
    angles = positions.astype(jnp.float32)[:, None] * frequency[None, :]
    cosine = jnp.concatenate([jnp.cos(angles), jnp.cos(angles)], axis=-1)[:, None, :]
    sine_table = jnp.concatenate([jnp.sin(angles), jnp.sin(angles)], axis=-1)[:, None, :]
    return (cosine, sine_table)

def rotate(values, cosine, sine_table):
    half_dim = values.shape[-1] // 2
    turned = jnp.concatenate([-values[..., half_dim:], values[..., :half_dim]], axis=-1)
    return values * cosine + turned * sine_table

def attend_block(query_block, frame_query, clip_query, all_keys, all_values, key_frame, key_clip):
    scores = jnp.einsum('qhd,khd->hqk', query_block, all_keys, precision=highest) * HEAD_DIM ** (-0.5)
    scores = low_back(scores)
    allowed = (clip_query[:, None] == key_clip[None, :]) & (key_frame[None, :] <= frame_query[:, None])
    scores = jnp.where(allowed[None], scores, -1e+30)
    row_max = lax.optimization_barrier(jnp.max(scores, axis=-1, keepdims=True))
    weights_exp = jnp.exp(scores - row_max)
    probabilities = weights_exp / lax.optimization_barrier(jnp.sum(weights_exp, axis=-1, keepdims=True))
    return jnp.einsum('hqk,khd->qhd', low(probabilities), all_values, precision=highest)

def pack_forward(tokens_in, weights, noise_rows, frame_of, clip_token):
    w_mod, b_mod, w_qkv, w_out, w_up, w_down = weights
    cond = low(jax.nn.silu(noise_rows))
    modulation = jnp.dot(cond, w_mod, precision=highest) + b_mod
    per_token = jnp.take(modulation, frame_of, axis=0)
    shift_one, scale_one, gate_one, shift_two, scale_two, gate_two = jnp.split(per_token, 6, axis=1)
    attn_in = low(normalized(tokens_in) * (1.0 + scale_one) + shift_one)
    projected = jnp.einsum('sd,dcf->scf', attn_in, w_qkv, precision=highest)
    cosine, sine_table = rotary(jnp.arange(SEQ, dtype=jnp.int32))
    q_raw = low_back(projected[:, 0]).reshape(SEQ, HEADS, HEAD_DIM)
    k_raw = low_back(projected[:, 1]).reshape(SEQ, HEADS, HEAD_DIM)
    queries = low(rotate(q_raw, cosine, sine_table))
    all_keys = low(rotate(k_raw, cosine, sine_table))
    all_values = low_back(low(projected[:, 2])).reshape(SEQ, HEADS, HEAD_DIM)
    block_rows = min(512, SEQ)
    block_count = SEQ // block_rows
    checked = jax.checkpoint(attend_block)

    def one_block(block_items):
        return checked(block_items[0], block_items[1], block_items[2], all_keys, all_values, frame_of, clip_token)
    attn = lax.map(one_block, (queries.reshape(block_count, block_rows, HEADS, HEAD_DIM), frame_of.reshape(block_count, block_rows), clip_token.reshape(block_count, block_rows)))
    attn = low_back(low(attn.reshape(SEQ, D)))
    branch_one = low_back(jnp.dot(attn, w_out, precision=highest))
    mixed_one = tokens_in + gate_one * branch_one
    mlp_in = low(normalized(mixed_one) * (1.0 + scale_two) + shift_two)
    pre = low_back(jnp.dot(mlp_in, w_up, precision=highest))
    hidden = low(jax.nn.gelu(pre, approximate=True))
    branch_two = low_back(jnp.dot(hidden, w_down, precision=highest))
    return mixed_one + gate_two * branch_two

def reference(tokens, cotangent, bucket, clip_of_frame, noise_index, noise_table, w_mod, b_mod, w_qkv, w_out, w_up, w_down):
    params = tuple((weight.astype(jnp.float32) for weight in (w_mod, b_mod, w_qkv, w_out, w_up, w_down)))
    positions = jnp.arange(SEQ, dtype=jnp.int32)

    def one_pack(totals, inputs):
        pack_tokens, pack_grad, grid_kind, clip_row, level_row = inputs
        frame_size = jnp.where(grid_kind == 0, FRAME_SMALL, FRAME_LARGE).astype(jnp.int32)
        frame_of = (positions // frame_size).astype(jnp.int32)
        clip_token = jnp.take(clip_row, frame_of)
        noise_rows = jnp.take(noise_table, level_row, axis=0).astype(jnp.float32)

        def forward(tokens_in, *weights):
            return pack_forward(tokens_in, weights, noise_rows, frame_of, clip_token)
        result, pullback = jax.vjp(forward, pack_tokens.reshape(SEQ, D).astype(jnp.float32), *params)
        gradients = pullback(pack_grad.reshape(SEQ, D).astype(jnp.float32))
        new_totals = tuple((total + grad for total, grad in zip(totals, gradients[1:])))
        return (new_totals, (result.astype(jnp.bfloat16).reshape(N_FRAMES, SHARD_TOK, D), gradients[0].astype(jnp.bfloat16).reshape(N_FRAMES, SHARD_TOK, D)))
    zeros = tuple((jnp.zeros_like(weight) for weight in params))
    totals, stacked = lax.scan(one_pack, zeros, (tokens, cotangent, bucket, clip_of_frame, noise_index))
    return (stacked[0], stacked[1], totals[0], totals[1], totals[2], totals[3], totals[4], totals[5])
```

```python
import functools

import jax
import jax.numpy as jnp
from jax import lax
from jax.experimental import pallas as pl
from jax.experimental.pallas import tpu as pltpu
from jax.sharding import PartitionSpec as P

HEAD_DIM = 64
FRAME_SMALL = 256
FRAME_LARGE = 1024
BLOCK = 256
LOG2E = 1.4426950408889634
SCALE = HEAD_DIM ** (-0.5)

eps = 1e-06
highest = lax.Precision.HIGHEST
f32 = jnp.float32
bf16 = jnp.bfloat16


def normalize(values):
    centre = values - jnp.mean(values, axis=-1, keepdims=True)
    spread = jnp.mean(centre * centre, axis=-1, keepdims=True)
    inverse = lax.rsqrt(spread + eps)
    return (centre * inverse, inverse)


def norm_back(grad, normed, inverse):
    mean_grad = jnp.mean(grad, axis=-1, keepdims=True)
    mean_mix = jnp.mean(grad * normed, axis=-1, keepdims=True)
    return inverse * (grad - mean_grad - normed * mean_mix)


def rotary_tables(positions, width):
    half_dim = HEAD_DIM // 2
    frequency = 10000.0 ** (-(jnp.arange(half_dim, dtype=f32) * 2.0 / HEAD_DIM))
    angles = positions.astype(f32)[:, None] * frequency[None, :]
    cosine = jnp.cos(angles)
    sine = jnp.sin(angles)
    copies = width // HEAD_DIM
    return (
        jnp.concatenate([cosine, cosine] * copies, axis=-1),
        jnp.concatenate([-sine, sine] * copies, axis=-1),
    )


def turn(values):
    half = HEAD_DIM // 2
    width = values.shape[-1]
    if width % 128 == 0:
        lane = lax.broadcasted_iota(jnp.int32, values.shape, 1)
        first = (lane % HEAD_DIM) < half
        return jnp.where(
            first, pltpu.roll(values, width - half, 1), pltpu.roll(values, half, 1)
        )
    pieces = []
    for at in range(0, width, HEAD_DIM):
        pieces += [values[:, at + half : at + HEAD_DIM], values[:, at : at + half]]
    return jnp.concatenate(pieces, axis=-1)


def project_kernel(frame_ref, x_ref, mod_ref, w_ref, cos_ref, sin_ref, in_ref, out_ref):
    block = pl.program_id(0)
    width = x_ref.shape[1]
    group = cos_ref.shape[1]
    row = mod_ref[pl.ds(frame_ref[block], 1), :]
    normed, _ = normalize(x_ref[...].astype(f32))
    attn_in = (normed * (1.0 + row[:, width : 2 * width]) + row[:, :width]).astype(bf16)
    in_ref[...] = attn_in
    projected = jnp.dot(attn_in, w_ref[...], preferred_element_type=f32)
    cosine, sine = cos_ref[...], sin_ref[...]
    for side in range(2):
        for kind in range(3):
            at = (side * 3 + kind) * group
            part = projected[:, at : at + group]
            if kind < 2:
                part = part * cosine + turn(part) * sine
            out_ref[side, kind] = part.astype(bf16)


def project(frames, tokens, mod, weights, cosine, sine):
    rows, width = tokens.shape
    columns = weights.shape[1]
    group = cosine.shape[1]
    whole = lambda i, fr: (0, 0)
    return pl.pallas_call(
        project_kernel,
        grid_spec=pltpu.PrefetchScalarGridSpec(
            num_scalar_prefetch=1,
            grid=(rows // BLOCK,),
            in_specs=[
                pl.BlockSpec((BLOCK, width), lambda i, fr: (i, 0)),
                pl.BlockSpec(mod.shape, whole),
                pl.BlockSpec((width, columns), whole),
                pl.BlockSpec((BLOCK, group), lambda i, fr: (i, 0)),
                pl.BlockSpec((BLOCK, group), lambda i, fr: (i, 0)),
            ],
            out_specs=[
                pl.BlockSpec((BLOCK, width), lambda i, fr: (i, 0)),
                pl.BlockSpec((2, 3, BLOCK, group), lambda i, fr: (0, 0, i, 0)),
            ],
        ),
        out_shape=[
            jax.ShapeDtypeStruct((rows, width), bf16),
            jax.ShapeDtypeStruct((2, 3, rows, group), bf16),
        ],
        name="project",
    )(frames, tokens, mod, weights, cosine, sine)


def only_head(values, head, axis):
    place = lax.broadcasted_iota(jnp.int32, values.shape, axis) // HEAD_DIM
    return jnp.where(place == head, values, jnp.zeros_like(values))


def key_loop(lo_ref, hi_ref, flag_ref, block, body, carry):
    lo, hi = lo_ref[block], hi_ref[block]
    big = flag_ref[0]
    wide = 2 * BLOCK
    count = (hi - lo) // 2

    def wide_step(j, c):
        return body(pl.multiple_of((lo + 2 * j) * BLOCK, BLOCK), wide, c)

    def last_step(j, c):
        return body(pl.multiple_of((lo + 2 * count + j) * BLOCK, BLOCK), BLOCK, c)

    carry = lax.fori_loop(0, count, wide_step, carry)
    return lax.fori_loop(0, (hi - lo) - 2 * count, last_step, carry)


def attend_kernel(lo_ref, hi_ref, flag_ref, q_ref, k_ref, v_ref, o_ref, lse_ref, vt_ref):
    block = pl.program_id(0)
    group = q_ref.shape[-1]
    heads = group // HEAD_DIM

    @pl.when(block == 0)
    def _():
        for at in range(0, v_ref.shape[1], BLOCK):
            vt_ref[:, at : at + BLOCK] = v_ref[0, at : at + BLOCK, :].T

    query = q_ref[0] * SCALE
    masked = [only_head(query, head, 1).astype(bf16) for head in range(heads)]

    def body(start, size, carry):
        keys = k_ref[0, pl.ds(start, size), :]
        result = []
        for head in range(heads):
            top, total, acc = carry[head]
            scores = (
                lax.dot_general(
                    keys, masked[head], (((1,), (1,)), ((), ())), preferred_element_type=f32
                )
                * LOG2E
            )
            new_top = jnp.maximum(top, jnp.max(scores, axis=0, keepdims=True))
            weight = jnp.exp2(scores - new_top)
            shrink = jnp.exp2(top - new_top)
            total = total * shrink + jnp.sum(weight, axis=0, keepdims=True)
            values = vt_ref[head * HEAD_DIM : (head + 1) * HEAD_DIM, pl.ds(start, size)]
            acc = acc * shrink + jnp.dot(values, weight.astype(bf16), preferred_element_type=f32)
            result.append((new_top, total, acc))
        return tuple(result)

    start = tuple(
        (
            jnp.full((1, BLOCK), -1e30, f32),
            jnp.zeros((1, BLOCK), f32),
            jnp.zeros((HEAD_DIM, BLOCK), f32),
        )
        for _ in range(heads)
    )
    final = key_loop(lo_ref, hi_ref, flag_ref, block, body, start)
    for head in range(heads):
        top, total, acc = final[head]
        o_ref[0, head * HEAD_DIM : (head + 1) * HEAD_DIM, :] = (acc / total).astype(bf16)
        lse_ref[0, head : head + 1, :] = top + jnp.log2(total)


def attend(lo, hi, flag, qkv, out_order):
    _, length, group = qkv.shape
    blocks = length // BLOCK
    return pl.pallas_call(
        attend_kernel,
        grid_spec=pltpu.PrefetchScalarGridSpec(
            num_scalar_prefetch=3,
            grid=(blocks,),
            in_specs=[
                pl.BlockSpec((1, BLOCK, group), lambda i, *s: (0, i, 0)),
                pl.BlockSpec((1, length, group), lambda i, *s: (1, 0, 0)),
                pl.BlockSpec((1, length, group), lambda i, *s: (2, 0, 0)),
            ],
            out_specs=[
                pl.BlockSpec((1, group, BLOCK), lambda i, *s: (out_order(i), 0, 0)),
                pl.BlockSpec((1, 8, BLOCK), lambda i, *s: (i, 0, 0)),
            ],
            scratch_shapes=[pltpu.VMEM((group, length), bf16)],
        ),
        out_shape=[
            jax.ShapeDtypeStruct((blocks, group, BLOCK), bf16),
            jax.ShapeDtypeStruct((blocks, 8, BLOCK), f32),
        ],
        name="attend",
    )(lo, hi, flag, qkv, qkv, qkv)


def attend_back_kernel(
    lo_ref,
    hi_ref,
    flag_ref,
    q_ref,
    k_ref,
    v_ref,
    o_ref,
    do_ref,
    lse_ref,
    cos_ref,
    sin_ref,
    out_ref,
    kt_ref,
    dk_ref,
    dv_ref,
):
    block = pl.program_id(0)
    length = k_ref.shape[1]
    group = q_ref.shape[-1]
    heads = group // HEAD_DIM

    @pl.when(block == 0)
    def _():
        dk_ref[...] = jnp.zeros_like(dk_ref)
        dv_ref[...] = jnp.zeros_like(dv_ref)
        for at in range(0, length, BLOCK):
            kt_ref[:, at : at + BLOCK] = k_ref[0, at : at + BLOCK, :].T

    query = q_ref[0] * SCALE
    grad_t = do_ref[0]
    grad = grad_t.T
    mixed = grad_t.astype(f32) * o_ref[0].astype(f32)
    query_m = jnp.concatenate([only_head(query, h, 1).astype(bf16) for h in range(heads)], axis=0)
    grad_m = jnp.concatenate([only_head(grad, h, 1).astype(bf16) for h in range(heads)], axis=0)
    grad_tm = [only_head(grad_t, h, 0).astype(bf16) for h in range(heads)]
    centre = [
        jnp.sum(mixed[h * HEAD_DIM : (h + 1) * HEAD_DIM], axis=0, keepdims=True)
        for h in range(heads)
    ]
    level = [lse_ref[0, h : h + 1, :] for h in range(heads)]

    def body(start, size, carry):
        keys = k_ref[0, pl.ds(start, size), :]
        values = v_ref[0, pl.ds(start, size), :]
        probs, grads, result = [], [], []
        for head in range(heads):
            rows = slice(head * BLOCK, (head + 1) * BLOCK)
            scores = lax.dot_general(
                keys, query_m[rows], (((1,), (1,)), ((), ())), preferred_element_type=f32
            )
            prob = jnp.exp2(scores * LOG2E - level[head])
            grad_prob = jnp.dot(values, grad_tm[head], preferred_element_type=f32)
            grad_score = (prob * (grad_prob - centre[head])).astype(bf16)
            probs.append(prob.astype(bf16))
            grads.append(grad_score)
            keys_t = kt_ref[head * HEAD_DIM : (head + 1) * HEAD_DIM, pl.ds(start, size)]
            result.append(
                carry[head] + jnp.dot(keys_t, grad_score, preferred_element_type=f32)
            )
        dv_ref[pl.ds(start, size), :] += jnp.dot(
            jnp.concatenate(probs, axis=1), grad_m, preferred_element_type=f32
        )
        dk_ref[pl.ds(start, size), :] += jnp.dot(
            jnp.concatenate(grads, axis=1), query_m, preferred_element_type=f32
        )
        return tuple(result)

    begin = tuple(jnp.zeros((HEAD_DIM, BLOCK), f32) for _ in range(heads))
    final = key_loop(lo_ref, hi_ref, flag_ref, block, body, begin)
    grad_query = (jnp.concatenate(final, axis=0) * SCALE).T
    here = pl.ds(pl.multiple_of(block * BLOCK, BLOCK), BLOCK)
    cosine, sine = cos_ref[here, :], sin_ref[here, :]
    out_ref[0, here, :] = (grad_query * cosine - turn(grad_query) * sine).astype(bf16)

    @pl.when(block == pl.num_programs(0) - 1)
    def _():
        for at in range(0, length, BLOCK):
            part = slice(at, at + BLOCK)
            grad_key = dk_ref[part, :]
            out_ref[1, part, :] = (
                grad_key * cos_ref[part, :] - turn(grad_key) * sin_ref[part, :]
            ).astype(bf16)
            out_ref[2, part, :] = dv_ref[part, :].astype(bf16)


def attend_back(lo, hi, flag, qkv, mixed, grad_mixed, level, cosine, sine, out_order):
    _, length, group = qkv.shape
    blocks = length // BLOCK
    whole = lambda i, *s: (0, 0)
    return pl.pallas_call(
        attend_back_kernel,
        grid_spec=pltpu.PrefetchScalarGridSpec(
            num_scalar_prefetch=3,
            grid=(blocks,),
            in_specs=[
                pl.BlockSpec((1, BLOCK, group), lambda i, *s: (0, i, 0)),
                pl.BlockSpec((1, length, group), lambda i, *s: (1, 0, 0)),
                pl.BlockSpec((1, length, group), lambda i, *s: (2, 0, 0)),
                pl.BlockSpec((1, group, BLOCK), lambda i, *s: (out_order(i), 0, 0)),
                pl.BlockSpec((1, group, BLOCK), lambda i, *s: (out_order(i), 0, 0)),
                pl.BlockSpec((1, 8, BLOCK), lambda i, *s: (i, 0, 0)),
                pl.BlockSpec((length, group), whole),
                pl.BlockSpec((length, group), whole),
            ],
            out_specs=pl.BlockSpec((3, length, group), lambda i, *s: (0, 0, 0)),
            scratch_shapes=[
                pltpu.VMEM((group, length), bf16),
                pltpu.VMEM((length, group), f32),
                pltpu.VMEM((length, group), f32),
            ],
        ),
        out_shape=jax.ShapeDtypeStruct((3, length, group), bf16),
        name="attend_back",
    )(lo, hi, flag, qkv, qkv, qkv, mixed, grad_mixed, level, cosine, sine)


def mm(left, right, contract_left, contract_right):
    return lax.dot_general(
        left,
        right,
        (((contract_left,), (contract_right,)), ((), ())),
        preferred_element_type=f32,
    )


def swap(value):
    return lax.ppermute(value, "frames", [(0, 1), (1, 0)])


def local(
    tokens,
    cotangent,
    bucket,
    clip_of_frame,
    noise_index,
    noise_table,
    w_mod,
    b_mod,
    w_qkv,
    w_out,
    w_up,
    w_down,
):
    tz = lax.axis_size("tensor")
    nb = lax.axis_size("batch")
    z = lax.axis_index("tensor")
    f = lax.axis_index("frames")
    b = lax.axis_index("batch")
    rows, width = tokens.shape[2], tokens.shape[3]
    shard_rows = rows * tz
    length = 2 * shard_rows
    width_local = w_qkv.shape[2]
    group = width_local // 2
    frame_slots = clip_of_frame.shape[1]
    hidden_local = w_up.shape[1]
    half = hidden_local // 2
    quarter = half // nb
    blocks = length // BLOCK

    tokens_local = tokens[0, 0]
    grad_out_local = cotangent[0, 0]

    unit = jnp.where(bucket[0] == 0, FRAME_SMALL // BLOCK, FRAME_LARGE // BLOCK).astype(jnp.int32)
    block_index = jnp.arange(blocks, dtype=jnp.int32)
    block_frame = block_index // unit
    clip_row = clip_of_frame[0]
    frame_ids = jnp.arange(frame_slots, dtype=jnp.int32)
    frame_clip = jnp.sum(
        jnp.where(block_frame[:, None] == frame_ids[None, :], clip_row[None, :], 0), axis=1
    )
    first_block = jnp.min(
        jnp.where(
            frame_clip[:, None] == frame_clip[None, :], block_index[None, :], jnp.int32(blocks)
        ),
        axis=1,
    )
    lo = first_block.astype(jnp.int32)
    hi = ((block_frame + 1) * unit).astype(jnp.int32)
    flag = bucket.astype(jnp.int32)

    all_bucket = lax.all_gather(
        jnp.concatenate([bucket, noise_index[0]]).astype(jnp.int32), "batch", axis=0
    )
    levels = jnp.take(noise_table, all_bucket[:, 1:].reshape(-1), axis=0)
    cond_all = jax.nn.silu(levels).astype(bf16).reshape(nb, frame_slots, width)
    cond = jax.nn.silu(jnp.take(noise_table, noise_index[0], axis=0)).astype(bf16)
    mod_part = jnp.dot(cond, w_mod, preferred_element_type=f32) + b_mod.astype(f32)[None, :]

    tokens_all = lax.all_gather(tokens_local, "tensor", axis=0, tiled=True)
    mod_whole = lax.all_gather(mod_part, "tensor", axis=1, tiled=True)

    own_frames = lax.dynamic_slice(block_frame, (f * tz,), (tz,))
    local_frame = lax.dynamic_index_in_dim(own_frames, z, keepdims=False)
    mod_row = lax.dynamic_slice(mod_whole, (local_frame, 0), (1, 6 * width))
    part = lambda at: mod_row[:, at * width : (at + 1) * width]
    shift_one, scale_one, gate_one, shift_two, scale_two, gate_two = map(part, range(6))

    w_pair = w_qkv.reshape(width, 3, 2, group)
    mine = lax.dynamic_index_in_dim(w_pair, f, axis=2, keepdims=False)
    theirs = lax.dynamic_index_in_dim(w_pair, 1 - f, axis=2, keepdims=False)
    w_arranged = jnp.concatenate(
        [mine.reshape(width, 3 * group), theirs.reshape(width, 3 * group)], axis=1
    )

    start = f * half + b * quarter
    up_piece = lax.dynamic_slice(w_up.T, (start, 0), (quarter, width))
    down_piece = lax.dynamic_slice(w_down, (start, 0), (quarter, width))
    pieces = jnp.stack([up_piece, down_piece])
    gathered = lax.all_gather(pieces, ("batch", "tensor"), axis=1, tiled=True)
    up_t, down = gathered[0], gathered[1]
    out_whole = lax.all_gather(w_out, "tensor", axis=0, tiled=True)

    cos_all, sin_all = rotary_tables(jnp.arange(length, dtype=jnp.int32), group)
    cos_own = lax.dynamic_slice(cos_all, (f * shard_rows, 0), (shard_rows, group))
    sin_own = lax.dynamic_slice(sin_all, (f * shard_rows, 0), (shard_rows, group))
    attn_in, qkv_pair = project(
        own_frames, tokens_all, mod_whole[:, : 2 * width], w_arranged, cos_own, sin_own
    )
    received = swap(qkv_pair[1])
    kept = qkv_pair[0]
    is_first = f == 0
    qkv = jnp.concatenate(
        [jnp.where(is_first, kept, received), jnp.where(is_first, received, kept)], axis=1
    )

    out_order = lambda i: (i % tz) * 2 + i // tz
    mixed, level = attend(lo, hi, flag, qkv, out_order)
    attn_t = lax.all_to_all(mixed, ("tensor", "frames"), 0, 0, tiled=True).reshape(width, rows)
    branch_one = mm(attn_t, out_whole, 0, 0)

    residual = tokens_local.astype(f32)
    normed_one, inverse_one = normalize(residual)
    mixed_one = residual + gate_one * branch_one
    normed_two, inverse_two = normalize(mixed_one)
    mlp_in = (normed_two * (1.0 + scale_two) + shift_two).astype(bf16)
    mlp_rows = jnp.concatenate([mlp_in, swap(mlp_in)], axis=0)
    grad_out = grad_out_local.astype(f32)
    grad_branch_two = (gate_two * grad_out).astype(bf16)
    grad_two_rows = jnp.concatenate([grad_branch_two, swap(grad_branch_two)], axis=0)

    pre = mm(mlp_rows, up_t, 1, 1)
    grad_hidden = mm(grad_two_rows, down, 1, 1)
    hidden_f32, gelu_pull = jax.vjp(lambda v: jax.nn.gelu(v, approximate=True), pre)
    hidden = hidden_f32.astype(bf16)
    grad_pre = gelu_pull(grad_hidden)[0].astype(bf16)
    grad_mlp_rows = mm(grad_pre, up_t, 1, 0)
    grad_mlp_in = grad_mlp_rows[:rows] + swap(grad_mlp_rows[rows:])
    branch_two_rows = mm(hidden, down, 1, 0)
    branch_two = branch_two_rows[:rows] + swap(branch_two_rows[rows:])
    result = (mixed_one + gate_two * branch_two).astype(bf16)
    grad_gate_two = grad_out * branch_two

    grad_down = mm(hidden, grad_two_rows, 0, 0).astype(bf16)
    grad_up_t = mm(grad_pre, mlp_rows, 0, 0).astype(bf16)

    grad_scale_two = grad_mlp_in * normed_two
    grad_mixed_one = grad_out + norm_back(grad_mlp_in * (1.0 + scale_two), normed_two, inverse_two)
    grad_branch_one = (gate_one * grad_mixed_one).astype(bf16)
    grad_gate_one = grad_mixed_one * branch_one

    grad_attn_t = mm(out_whole, grad_branch_one, 1, 1).astype(bf16)
    grad_mixed = lax.all_to_all(
        grad_attn_t.reshape(blocks, group, rows), ("tensor", "frames"), 0, 0, tiled=True
    )
    grad_out_weights = mm(attn_t, grad_branch_one, 1, 0).astype(bf16)

    grad_qkv = attend_back(
        lo, hi, flag, qkv, mixed, grad_mixed, level, cos_all, sin_all, out_order
    )
    grad_first, grad_second = grad_qkv[:, :shard_rows], grad_qkv[:, shard_rows:]
    grad_received = swap(jnp.where(is_first, grad_second, grad_first))
    grad_kept = jnp.where(is_first, grad_first, grad_second)
    grad_arranged = jnp.concatenate(
        [grad_kept[0], grad_kept[1], grad_kept[2]]
        + [grad_received[0], grad_received[1], grad_received[2]],
        axis=1,
    )
    grad_attn_part = mm(grad_arranged, w_arranged, 1, 1)

    normed_all, _ = normalize(tokens_all.astype(f32))
    blocked = grad_attn_part.reshape(tz, rows, width)
    sum_shift_one = jnp.sum(blocked, axis=1)
    sum_scale_one = jnp.sum(blocked * normed_all.reshape(tz, rows, width), axis=1)
    local_sums = jnp.concatenate(
        [
            jnp.sum(v, axis=0)
            for v in (grad_gate_one, grad_mlp_in, grad_scale_two, grad_gate_two)
        ]
    )
    own_slot = (jnp.arange(tz, dtype=jnp.int32) == z).astype(f32)
    frame_sums = jnp.concatenate(
        [sum_shift_one, sum_scale_one, own_slot[:, None] * local_sums[None, :]], axis=1
    )
    share = lax.psum_scatter(frame_sums, "tensor", scatter_dimension=1, tiled=True)
    shares = lax.all_gather(share, ("batch", "frames"), axis=0, tiled=True)
    all_unit = jnp.where(
        all_bucket[:, 0] == 0, FRAME_SMALL // BLOCK, FRAME_LARGE // BLOCK
    ).astype(jnp.int32)
    all_frame = block_index[None, :] // all_unit[:, None]
    picked = (all_frame[:, :, None] == frame_ids[None, None, :]).astype(f32)
    cond_blocks = jnp.einsum("bif,bfd->bid", picked, cond_all.astype(f32), precision=highest)
    grad_w_mod = mm_highest(cond_blocks.reshape(nb * blocks, width), shares)
    grad_b_mod = jnp.sum(shares, axis=0)

    grad_attn_in = lax.psum_scatter(
        grad_attn_part.astype(bf16), "tensor", scatter_dimension=0, tiled=True
    ).astype(f32)
    grad_tokens = grad_mixed_one + norm_back(
        grad_attn_in * (1.0 + scale_one), normed_one, inverse_one
    )

    grad_w_arranged = mm(attn_in, grad_arranged, 0, 0)
    mine_grad = grad_w_arranged[:, : 3 * group].reshape(width, 3, 1, group)
    theirs_grad = grad_w_arranged[:, 3 * group :].reshape(width, 3, 1, group)
    grad_w_qkv = jnp.concatenate(
        [
            jnp.where(is_first, mine_grad, theirs_grad),
            jnp.where(is_first, theirs_grad, mine_grad),
        ],
        axis=2,
    ).reshape(width, 3, width_local)
    grad_w_qkv = lax.psum(grad_w_qkv.astype(bf16), ("frames", "batch")).astype(f32)
    grad_w_out = lax.psum(
        lax.psum_scatter(grad_out_weights, "tensor", scatter_dimension=0, tiled=True),
        ("frames", "batch"),
    ).astype(f32)

    def reduce_rows(grad):
        shard = lax.psum_scatter(grad, ("batch", "tensor"), scatter_dimension=0, tiled=True)
        return lax.all_gather(shard, ("frames", "batch"), axis=0, tiled=True).astype(f32)

    grad_w_down = reduce_rows(grad_down)
    grad_w_up = reduce_rows(grad_up_t).T
    return (
        result.reshape(1, 1, rows, width),
        grad_tokens.astype(bf16).reshape(1, 1, rows, width),
        grad_w_mod,
        grad_b_mod,
        grad_w_qkv,
        grad_w_out,
        grad_w_up,
        grad_w_down,
    )


def mm_highest(left, right):
    return lax.dot_general(left, right, (((0,), (0,)), ((), ())), precision=highest)


def solution(mesh):
    placed = (
        P("batch", "frames", "tensor", None),
        P("batch", "frames", "tensor", None),
        P("batch"),
        P("batch", None),
        P("batch", None),
        P(),
        P(None, "tensor"),
        P("tensor"),
        P(None, None, "tensor"),
        P("tensor", None),
        P(None, "tensor"),
        P("tensor", None),
    )
    return jax.shard_map(
        local,
        mesh=mesh,
        in_specs=placed,
        out_specs=(
            P("batch", "frames", "tensor", None),
            P("batch", "frames", "tensor", None),
            P(None, "tensor"),
            P("tensor"),
            P(None, None, "tensor"),
            P("tensor", None),
            P(None, "tensor"),
            P("tensor", None),
        ),
        check_vma=False,
    )
```

```python
import functools

import jax
import jax.numpy as jnp
from jax import lax
from jax.experimental import pallas as pl
from jax.experimental.pallas import tpu as pltpu
from jax.sharding import PartitionSpec as P

HEAD_DIM = 64
FRAME_SMALL = 256
FRAME_LARGE = 1024
BLOCK = 256
LOG2E = 1.4426950408889634
SCALE = HEAD_DIM ** (-0.5)

eps = 1e-06
highest = lax.Precision.HIGHEST
f32 = jnp.float32
bf16 = jnp.bfloat16


def normalize(values):
    centre = values - jnp.mean(values, axis=-1, keepdims=True)
    spread = jnp.mean(centre * centre, axis=-1, keepdims=True)
    inverse = lax.rsqrt(spread + eps)
    return (centre * inverse, inverse)


def norm_back(grad, normed, inverse):
    mean_grad = jnp.mean(grad, axis=-1, keepdims=True)
    mean_mix = jnp.mean(grad * normed, axis=-1, keepdims=True)
    return inverse * (grad - mean_grad - normed * mean_mix)


def rotary_tables(positions, width):
    half_dim = HEAD_DIM // 2
    frequency = 10000.0 ** (-(jnp.arange(half_dim, dtype=f32) * 2.0 / HEAD_DIM))
    angles = positions.astype(f32)[:, None] * frequency[None, :]
    cosine = jnp.cos(angles)
    sine = jnp.sin(angles)
    copies = width // HEAD_DIM
    return (
        jnp.concatenate([cosine, cosine] * copies, axis=-1),
        jnp.concatenate([-sine, sine] * copies, axis=-1),
    )


def turn(values):
    half = HEAD_DIM // 2
    width = values.shape[-1]
    if width % 128 == 0:
        lane = lax.broadcasted_iota(jnp.int32, values.shape, 1)
        first = (lane % HEAD_DIM) < half
        return jnp.where(
            first, pltpu.roll(values, width - half, 1), pltpu.roll(values, half, 1)
        )
    pieces = []
    for at in range(0, width, HEAD_DIM):
        pieces += [values[:, at + half : at + HEAD_DIM], values[:, at : at + half]]
    return jnp.concatenate(pieces, axis=-1)


def project_kernel(frame_ref, x_ref, mod_ref, w_ref, cos_ref, sin_ref, in_ref, out_ref):
    block = pl.program_id(0)
    width = x_ref.shape[1]
    group = cos_ref.shape[1]
    row = mod_ref[pl.ds(frame_ref[block], 1), :]
    normed, _ = normalize(x_ref[...].astype(f32))
    attn_in = (normed * (1.0 + row[:, width : 2 * width]) + row[:, :width]).astype(bf16)
    in_ref[...] = attn_in
    projected = jnp.dot(attn_in, w_ref[...], preferred_element_type=f32)
    cosine, sine = cos_ref[...], sin_ref[...]
    for side in range(2):
        for kind in range(3):
            at = (side * 3 + kind) * group
            part = projected[:, at : at + group]
            if kind < 2:
                part = part * cosine + turn(part) * sine
            out_ref[side, kind] = part.astype(bf16)


def project(frames, tokens, mod, weights, cosine, sine):
    rows, width = tokens.shape
    columns = weights.shape[1]
    group = cosine.shape[1]
    whole = lambda i, fr: (0, 0)
    return pl.pallas_call(
        project_kernel,
        grid_spec=pltpu.PrefetchScalarGridSpec(
            num_scalar_prefetch=1,
            grid=(rows // BLOCK,),
            in_specs=[
                pl.BlockSpec((BLOCK, width), lambda i, fr: (i, 0)),
                pl.BlockSpec(mod.shape, whole),
                pl.BlockSpec((width, columns), whole),
                pl.BlockSpec((BLOCK, group), lambda i, fr: (i, 0)),
                pl.BlockSpec((BLOCK, group), lambda i, fr: (i, 0)),
            ],
            out_specs=[
                pl.BlockSpec((BLOCK, width), lambda i, fr: (i, 0)),
                pl.BlockSpec((2, 3, BLOCK, group), lambda i, fr: (0, 0, i, 0)),
            ],
        ),
        out_shape=[
            jax.ShapeDtypeStruct((rows, width), bf16),
            jax.ShapeDtypeStruct((2, 3, rows, group), bf16),
        ],
        name="project",
    )(frames, tokens, mod, weights, cosine, sine)


def only_head(values, head, axis):
    place = lax.broadcasted_iota(jnp.int32, values.shape, axis) // HEAD_DIM
    return jnp.where(place == head, values, jnp.zeros_like(values))


def key_loop(lo_ref, hi_ref, flag_ref, block, body, carry):
    lo, hi = lo_ref[block], hi_ref[block]
    big = flag_ref[0]
    wide = 2 * BLOCK
    count = (hi - lo) // 2

    def wide_step(j, c):
        return body(pl.multiple_of((lo + 2 * j) * BLOCK, BLOCK), wide, c)

    def last_step(j, c):
        return body(pl.multiple_of((lo + 2 * count + j) * BLOCK, BLOCK), BLOCK, c)

    carry = lax.fori_loop(0, count, wide_step, carry)
    return lax.fori_loop(0, (hi - lo) - 2 * count, last_step, carry)


def attend_kernel(lo_ref, hi_ref, flag_ref, q_ref, k_ref, v_ref, o_ref, lse_ref, vt_ref):
    block = pl.program_id(0)
    group = q_ref.shape[-1]
    heads = group // HEAD_DIM

    @pl.when(block == 0)
    def _():
        for at in range(0, v_ref.shape[1], BLOCK):
            vt_ref[:, at : at + BLOCK] = v_ref[0, at : at + BLOCK, :].T

    query = q_ref[0] * SCALE
    masked = [only_head(query, head, 1).astype(bf16) for head in range(heads)]

    def body(start, size, carry):
        keys = k_ref[0, pl.ds(start, size), :]
        result = []
        for head in range(heads):
            top, total, acc = carry[head]
            scores = (
                lax.dot_general(
                    keys, masked[head], (((1,), (1,)), ((), ())), preferred_element_type=f32
                )
                * LOG2E
            )
            new_top = jnp.maximum(top, jnp.max(scores, axis=0, keepdims=True))
            weight = jnp.exp2(scores - new_top)
            shrink = jnp.exp2(top - new_top)
            total = total * shrink + jnp.sum(weight, axis=0, keepdims=True)
            values = vt_ref[head * HEAD_DIM : (head + 1) * HEAD_DIM, pl.ds(start, size)]
            acc = acc * shrink + jnp.dot(values, weight.astype(bf16), preferred_element_type=f32)
            result.append((new_top, total, acc))
        return tuple(result)

    start = tuple(
        (
            jnp.full((1, BLOCK), -1e30, f32),
            jnp.zeros((1, BLOCK), f32),
            jnp.zeros((HEAD_DIM, BLOCK), f32),
        )
        for _ in range(heads)
    )
    final = key_loop(lo_ref, hi_ref, flag_ref, block, body, start)
    for head in range(heads):
        top, total, acc = final[head]
        o_ref[0, head * HEAD_DIM : (head + 1) * HEAD_DIM, :] = (acc / total).astype(bf16)
        lse_ref[0, head : head + 1, :] = top + jnp.log2(total)


def attend(lo, hi, flag, qkv, out_order):
    _, length, group = qkv.shape
    blocks = length // BLOCK
    return pl.pallas_call(
        attend_kernel,
        grid_spec=pltpu.PrefetchScalarGridSpec(
            num_scalar_prefetch=3,
            grid=(blocks,),
            in_specs=[
                pl.BlockSpec((1, BLOCK, group), lambda i, *s: (0, i, 0)),
                pl.BlockSpec((1, length, group), lambda i, *s: (1, 0, 0)),
                pl.BlockSpec((1, length, group), lambda i, *s: (2, 0, 0)),
            ],
            out_specs=[
                pl.BlockSpec((1, group, BLOCK), lambda i, *s: (out_order(i), 0, 0)),
                pl.BlockSpec((1, 8, BLOCK), lambda i, *s: (i, 0, 0)),
            ],
            scratch_shapes=[pltpu.VMEM((group, length), bf16)],
        ),
        out_shape=[
            jax.ShapeDtypeStruct((blocks, group, BLOCK), bf16),
            jax.ShapeDtypeStruct((blocks, 8, BLOCK), f32),
        ],
        name="attend",
    )(lo, hi, flag, qkv, qkv, qkv)


def attend_back_kernel(
    lo_ref,
    hi_ref,
    flag_ref,
    q_ref,
    k_ref,
    v_ref,
    o_ref,
    do_ref,
    lse_ref,
    cos_ref,
    sin_ref,
    out_ref,
    kt_ref,
    dk_ref,
    dv_ref,
):
    block = pl.program_id(0)
    length = k_ref.shape[1]
    group = q_ref.shape[-1]
    heads = group // HEAD_DIM

    @pl.when(block == 0)
    def _():
        dk_ref[...] = jnp.zeros_like(dk_ref)
        dv_ref[...] = jnp.zeros_like(dv_ref)
        for at in range(0, length, BLOCK):
            kt_ref[:, at : at + BLOCK] = k_ref[0, at : at + BLOCK, :].T

    query = q_ref[0] * SCALE
    grad_t = do_ref[0]
    grad = grad_t.T
    mixed = grad_t.astype(f32) * o_ref[0].astype(f32)
    query_m = jnp.concatenate([only_head(query, h, 1).astype(bf16) for h in range(heads)], axis=0)
    grad_m = jnp.concatenate([only_head(grad, h, 1).astype(bf16) for h in range(heads)], axis=0)
    grad_tm = [only_head(grad_t, h, 0).astype(bf16) for h in range(heads)]
    centre = [
        jnp.sum(mixed[h * HEAD_DIM : (h + 1) * HEAD_DIM], axis=0, keepdims=True)
        for h in range(heads)
    ]
    level = [lse_ref[0, h : h + 1, :] for h in range(heads)]

    def body(start, size, carry):
        keys = k_ref[0, pl.ds(start, size), :]
        values = v_ref[0, pl.ds(start, size), :]
        probs, grads, result = [], [], []
        for head in range(heads):
            rows = slice(head * BLOCK, (head + 1) * BLOCK)
            scores = lax.dot_general(
                keys, query_m[rows], (((1,), (1,)), ((), ())), preferred_element_type=f32
            )
            prob = jnp.exp2(scores * LOG2E - level[head])
            grad_prob = jnp.dot(values, grad_tm[head], preferred_element_type=f32)
            grad_score = (prob * (grad_prob - centre[head])).astype(bf16)
            probs.append(prob.astype(bf16))
            grads.append(grad_score)
            keys_t = kt_ref[head * HEAD_DIM : (head + 1) * HEAD_DIM, pl.ds(start, size)]
            result.append(
                carry[head] + jnp.dot(keys_t, grad_score, preferred_element_type=f32)
            )
        dv_ref[pl.ds(start, size), :] += jnp.dot(
            jnp.concatenate(probs, axis=1), grad_m, preferred_element_type=f32
        )
        dk_ref[pl.ds(start, size), :] += jnp.dot(
            jnp.concatenate(grads, axis=1), query_m, preferred_element_type=f32
        )
        return tuple(result)

    begin = tuple(jnp.zeros((HEAD_DIM, BLOCK), f32) for _ in range(heads))
    final = key_loop(lo_ref, hi_ref, flag_ref, block, body, begin)
    grad_query = (jnp.concatenate(final, axis=0) * SCALE).T
    here = pl.ds(pl.multiple_of(block * BLOCK, BLOCK), BLOCK)
    cosine, sine = cos_ref[here, :], sin_ref[here, :]
    out_ref[0, here, :] = (grad_query * cosine - turn(grad_query) * sine).astype(bf16)

    @pl.when(block == pl.num_programs(0) - 1)
    def _():
        for at in range(0, length, BLOCK):
            part = slice(at, at + BLOCK)
            grad_key = dk_ref[part, :]
            out_ref[1, part, :] = (
                grad_key * cos_ref[part, :] - turn(grad_key) * sin_ref[part, :]
            ).astype(bf16)
            out_ref[2, part, :] = dv_ref[part, :].astype(bf16)


def attend_back(lo, hi, flag, qkv, mixed, grad_mixed, level, cosine, sine, out_order):
    _, length, group = qkv.shape
    blocks = length // BLOCK
    whole = lambda i, *s: (0, 0)
    return pl.pallas_call(
        attend_back_kernel,
        grid_spec=pltpu.PrefetchScalarGridSpec(
            num_scalar_prefetch=3,
            grid=(blocks,),
            in_specs=[
                pl.BlockSpec((1, BLOCK, group), lambda i, *s: (0, i, 0)),
                pl.BlockSpec((1, length, group), lambda i, *s: (1, 0, 0)),
                pl.BlockSpec((1, length, group), lambda i, *s: (2, 0, 0)),
                pl.BlockSpec((1, group, BLOCK), lambda i, *s: (out_order(i), 0, 0)),
                pl.BlockSpec((1, group, BLOCK), lambda i, *s: (out_order(i), 0, 0)),
                pl.BlockSpec((1, 8, BLOCK), lambda i, *s: (i, 0, 0)),
                pl.BlockSpec((length, group), whole),
                pl.BlockSpec((length, group), whole),
            ],
            out_specs=pl.BlockSpec((3, length, group), lambda i, *s: (0, 0, 0)),
            scratch_shapes=[
                pltpu.VMEM((group, length), bf16),
                pltpu.VMEM((length, group), f32),
                pltpu.VMEM((length, group), f32),
            ],
        ),
        out_shape=jax.ShapeDtypeStruct((3, length, group), bf16),
        name="attend_back",
    )(lo, hi, flag, qkv, qkv, qkv, mixed, grad_mixed, level, cosine, sine)


def mm(left, right, contract_left, contract_right):
    return lax.dot_general(
        left,
        right,
        (((contract_left,), (contract_right,)), ((), ())),
        preferred_element_type=f32,
    )


def swap(value):
    return lax.ppermute(value, "frames", [(0, 1), (1, 0)])


def paired(value, axis, step):
    count = lax.axis_size(axis)
    return lax.ppermute(value, axis, [(i, i ^ step) for i in range(count)])


def direct():
    return lax.axis_size("tensor") == 4 and lax.axis_size("batch") == 4


def gather_hidden(up_t, down):
    nb = lax.axis_size("batch")
    f, b = lax.axis_index("frames"), lax.axis_index("batch")
    half, width = up_t.shape[0] // 2, up_t.shape[1]
    quarter = half // nb
    if not direct():
        start = (f * half + b * quarter, 0)
        pieces = jnp.stack(
            [lax.dynamic_slice(v, start, (quarter, width)) for v in (up_t, down)]
        )
        gathered = lax.all_gather(pieces, ("batch", "tensor"), axis=1, tiled=True)
        return gathered[0], gathered[1]

    def own(values):
        return [
            lax.dynamic_slice(values, (f * half + (b ^ r) * quarter, 0), (quarter, width))
            for r in range(nb)
        ]

    ups, downs = own(up_t), own(down)
    piece = jnp.stack([ups[0], downs[0]])
    arrived = [paired(piece, "tensor", step) for step in (1, 2, 3)]
    for group in (arrived[:1], arrived[1:]):
        up = jnp.stack([v[0] for v in group])
        low = jnp.stack([v[1] for v in group])
        up_x = paired(up, "batch", 1)
        low_y = paired(low, "batch", 2)
        up_far = paired(jnp.stack([up, up_x]), "batch", 2)
        low_far = paired(jnp.stack([low, low_y]), "batch", 1)
        for at in range(len(group)):
            ups += [up[at], up_x[at], up_far[0, at], up_far[1, at]]
            downs += [low[at], low_far[0, at], low_y[at], low_far[1, at]]
    return jnp.concatenate(ups, axis=0), jnp.concatenate(downs, axis=0)


def collect_rows(partial, rows):
    z = lax.axis_index("tensor")
    tz = lax.axis_size("tensor")
    if tz & (tz - 1):
        return lax.psum_scatter(partial, "tensor", scatter_dimension=0, tiled=True).astype(f32)
    block = lambda at: lax.dynamic_slice(partial, (at * rows, 0), (rows, partial.shape[1]))
    total = block(z).astype(f32)
    for step in range(tz - 1, 0, -1):
        total = total + paired(block(z ^ step), "tensor", step).astype(f32)
    return total


def place_kernel(order_ref, up_ref, down_ref, up_out, down_out):
    up_out[...] = up_ref[0].astype(f32).T
    down_out[...] = down_ref[0].astype(f32)


def place(order, ups, downs):
    count, quarter, width = ups.shape
    return pl.pallas_call(
        place_kernel,
        grid_spec=pltpu.PrefetchScalarGridSpec(
            num_scalar_prefetch=1,
            grid=(count,),
            in_specs=[pl.BlockSpec((1, quarter, width), lambda i, o: (o[i], 0, 0))] * 2,
            out_specs=[
                pl.BlockSpec((width, quarter), lambda i, o: (0, i)),
                pl.BlockSpec((quarter, width), lambda i, o: (i, 0)),
            ],
        ),
        out_shape=[
            jax.ShapeDtypeStruct((width, count * quarter), f32),
            jax.ShapeDtypeStruct((count * quarter, width), f32),
        ],
        name="place",
    )(order, ups, downs)


def reduce_hidden(grad_up_t, grad_down):
    nb = lax.axis_size("batch")
    f, b = lax.axis_index("frames"), lax.axis_index("batch")
    width = grad_up_t.shape[1]
    if not direct():

        def reduce_rows(grad):
            shard = lax.psum_scatter(grad, ("batch", "tensor"), scatter_dimension=0, tiled=True)
            return lax.all_gather(shard, ("frames", "batch"), axis=0, tiled=True).astype(f32)

        return reduce_rows(grad_up_t).T, reduce_rows(grad_down)
    up = grad_up_t.reshape(4, nb, -1, width)
    down = grad_down.reshape(4, nb, -1, width)
    added = lambda v, w: (v.astype(f32) + w.astype(f32)).astype(bf16)
    parts = {}
    for group in ((2, 3), (0, 1)):
        at = slice(group[0], group[1] + 1)
        u, d = up[at], down[at]
        u_near = added(u[:, :2], paired(u[:, 2:], "batch", 2))
        d_sent = jnp.stack([d[:, 1], d[:, 3]], axis=1)
        d_kept = jnp.stack([d[:, 0], d[:, 2]], axis=1)
        d_near = added(d_kept, paired(d_sent, "batch", 1))
        u_sum = added(u_near[:, 0], paired(u_near[:, 1], "batch", 1))
        d_sum = added(d_near[:, 0], paired(d_near[:, 1], "batch", 2))
        for i, step in enumerate(group):
            parts[step] = jnp.stack([u_sum[i], d_sum[i]])
    total = parts[0].astype(f32)
    for step in (2, 3, 1):
        total = total + paired(parts[step], "tensor", step).astype(f32)
    u, d = total[0].astype(bf16), total[1].astype(bf16)
    u_x = paired(u, "batch", 1)
    d_y = paired(d, "batch", 2)
    u_far = paired(jnp.stack([u, u_x]), "batch", 2)
    d_far = paired(jnp.stack([d, d_y]), "batch", 1)
    u_half = jnp.stack([u, u_x, u_far[0], u_far[1]])
    d_half = jnp.stack([d, d_far[0], d_y, d_far[1]])
    other = swap(jnp.stack([u_half, d_half]))
    quarters = jnp.arange(nb, dtype=jnp.int32) ^ b
    order = jnp.concatenate(
        [jnp.where(f == 0, 0, nb) + quarters, jnp.where(f == 0, nb, 0) + quarters]
    ).astype(jnp.int32)
    return place(
        order,
        jnp.concatenate([u_half, other[0]], axis=0),
        jnp.concatenate([d_half, other[1]], axis=0),
    )


def local(
    tokens,
    cotangent,
    bucket,
    clip_of_frame,
    noise_index,
    noise_table,
    w_mod,
    b_mod,
    w_qkv,
    w_out,
    w_up,
    w_down,
):
    tz = lax.axis_size("tensor")
    nb = lax.axis_size("batch")
    z = lax.axis_index("tensor")
    f = lax.axis_index("frames")
    b = lax.axis_index("batch")
    rows, width = tokens.shape[2], tokens.shape[3]
    shard_rows = rows * tz
    length = 2 * shard_rows
    width_local = w_qkv.shape[2]
    group = width_local // 2
    frame_slots = clip_of_frame.shape[1]
    blocks = length // BLOCK

    tokens_local = tokens[0, 0]
    grad_out_local = cotangent[0, 0]

    unit = jnp.where(bucket[0] == 0, FRAME_SMALL // BLOCK, FRAME_LARGE // BLOCK).astype(jnp.int32)
    block_index = jnp.arange(blocks, dtype=jnp.int32)
    block_frame = block_index // unit
    clip_row = clip_of_frame[0]
    frame_ids = jnp.arange(frame_slots, dtype=jnp.int32)
    frame_clip = jnp.sum(
        jnp.where(block_frame[:, None] == frame_ids[None, :], clip_row[None, :], 0), axis=1
    )
    first_block = jnp.min(
        jnp.where(
            frame_clip[:, None] == frame_clip[None, :], block_index[None, :], jnp.int32(blocks)
        ),
        axis=1,
    )
    lo = first_block.astype(jnp.int32)
    hi = ((block_frame + 1) * unit).astype(jnp.int32)
    flag = bucket.astype(jnp.int32)

    all_bucket = lax.all_gather(
        jnp.concatenate([bucket, noise_index[0]]).astype(jnp.int32), "batch", axis=0
    )
    levels = jnp.take(noise_table, all_bucket[:, 1:].reshape(-1), axis=0)
    cond_all = jax.nn.silu(levels).astype(bf16).reshape(nb, frame_slots, width)
    cond = jax.nn.silu(jnp.take(noise_table, noise_index[0], axis=0)).astype(bf16)
    mod_part = jnp.dot(cond, w_mod, preferred_element_type=f32) + b_mod.astype(f32)[None, :]

    tokens_all = lax.all_gather(tokens_local, "tensor", axis=0, tiled=True)
    mod_whole = lax.all_gather(mod_part, "tensor", axis=1, tiled=True)

    all_unit = jnp.where(
        all_bucket[:, 0] == 0, FRAME_SMALL // BLOCK, FRAME_LARGE // BLOCK
    ).astype(jnp.int32)
    all_frame = block_index[None, :] // all_unit[:, None]
    picked = (all_frame[:, :, None] == frame_ids[None, None, :]).astype(f32)
    cond_blocks = jnp.einsum("bif,bfd->bid", picked, cond_all.astype(f32), precision=highest)
    mod_whole, cond_blocks = lax.optimization_barrier((mod_whole, cond_blocks))

    own_frames = lax.dynamic_slice(block_frame, (f * tz,), (tz,))
    local_frame = lax.dynamic_index_in_dim(own_frames, z, keepdims=False)
    mod_row = lax.dynamic_slice(mod_whole, (local_frame, 0), (1, 6 * width))
    part = lambda at: mod_row[:, at * width : (at + 1) * width]
    shift_one, scale_one, gate_one, shift_two, scale_two, gate_two = map(part, range(6))

    w_pair = w_qkv.reshape(width, 3, 2, group)
    mine = lax.dynamic_index_in_dim(w_pair, f, axis=2, keepdims=False)
    theirs = lax.dynamic_index_in_dim(w_pair, 1 - f, axis=2, keepdims=False)
    w_arranged = jnp.concatenate(
        [mine.reshape(width, 3 * group), theirs.reshape(width, 3 * group)], axis=1
    )

    up_t, down = gather_hidden(w_up.T, w_down)
    out_rows = w_out.shape[0] // (2 * nb)
    out_piece = lax.dynamic_slice(w_out, ((f * nb + b) * out_rows, 0), (out_rows, width))
    out_whole = lax.all_gather(out_piece, ("tensor", "frames", "batch"), axis=0, tiled=True)

    cos_all, sin_all = rotary_tables(jnp.arange(length, dtype=jnp.int32), group)
    cos_own = lax.dynamic_slice(cos_all, (f * shard_rows, 0), (shard_rows, group))
    sin_own = lax.dynamic_slice(sin_all, (f * shard_rows, 0), (shard_rows, group))
    attn_in, qkv_pair = project(
        own_frames, tokens_all, mod_whole[:, : 2 * width], w_arranged, cos_own, sin_own
    )
    received = swap(qkv_pair[1])
    kept = qkv_pair[0]
    is_first = f == 0
    qkv = jnp.concatenate(
        [jnp.where(is_first, kept, received), jnp.where(is_first, received, kept)], axis=1
    )

    out_order = lambda i: (i % tz) * 2 + i // tz
    mixed, level = attend(lo, hi, flag, qkv, out_order)
    attn_t = lax.all_to_all(mixed, ("tensor", "frames"), 0, 0, tiled=True).reshape(width, rows)
    branch_one = mm(attn_t, out_whole, 0, 0)

    residual = tokens_local.astype(f32)
    normed_one, inverse_one = normalize(residual)
    mixed_one = residual + gate_one * branch_one
    normed_two, inverse_two = normalize(mixed_one)
    mlp_in = (normed_two * (1.0 + scale_two) + shift_two).astype(bf16)
    mlp_rows = jnp.concatenate([mlp_in, swap(mlp_in)], axis=0)
    grad_out = grad_out_local.astype(f32)
    grad_branch_two = (gate_two * grad_out).astype(bf16)
    grad_two_rows = jnp.concatenate([grad_branch_two, swap(grad_branch_two)], axis=0)

    pre = mm(mlp_rows, up_t, 1, 1)
    grad_hidden = mm(grad_two_rows, down, 1, 1)
    hidden_f32, gelu_pull = jax.vjp(lambda v: jax.nn.gelu(v, approximate=True), pre)
    hidden = hidden_f32.astype(bf16)
    grad_pre = gelu_pull(grad_hidden)[0].astype(bf16)
    grad_mlp_rows = mm(grad_pre, up_t, 1, 0)
    grad_mlp_in = grad_mlp_rows[:rows] + swap(grad_mlp_rows[rows:])
    branch_two_rows = mm(hidden, down, 1, 0)
    branch_two = branch_two_rows[:rows] + swap(branch_two_rows[rows:])
    result = (mixed_one + gate_two * branch_two).astype(bf16)
    grad_gate_two = grad_out * branch_two

    grad_down = mm(hidden, grad_two_rows, 0, 0).astype(bf16)
    grad_up_t = mm(grad_pre, mlp_rows, 0, 0).astype(bf16)

    grad_scale_two = grad_mlp_in * normed_two
    grad_mixed_one = grad_out + norm_back(grad_mlp_in * (1.0 + scale_two), normed_two, inverse_two)
    grad_branch_one = (gate_one * grad_mixed_one).astype(bf16)
    grad_gate_one = grad_mixed_one * branch_one

    grad_attn_t = mm(out_whole, grad_branch_one, 1, 1).astype(bf16)
    grad_mixed = lax.all_to_all(
        grad_attn_t.reshape(blocks, group, rows), ("tensor", "frames"), 0, 0, tiled=True
    )
    grad_out_weights = mm(attn_t, grad_branch_one, 1, 0).astype(bf16)

    grad_qkv = attend_back(
        lo, hi, flag, qkv, mixed, grad_mixed, level, cos_all, sin_all, out_order
    )
    grad_first, grad_second = grad_qkv[:, :shard_rows], grad_qkv[:, shard_rows:]
    grad_received = swap(jnp.where(is_first, grad_second, grad_first))
    grad_kept = jnp.where(is_first, grad_first, grad_second)
    grad_arranged = jnp.concatenate(
        [grad_kept[0], grad_kept[1], grad_kept[2]]
        + [grad_received[0], grad_received[1], grad_received[2]],
        axis=1,
    )
    grad_attn_part = mm(grad_arranged, w_arranged, 1, 1)

    normed_all, _ = normalize(tokens_all.astype(f32))
    blocked = grad_attn_part.reshape(tz, rows, width)
    sum_shift_one = jnp.sum(blocked, axis=1)
    sum_scale_one = jnp.sum(blocked * normed_all.reshape(tz, rows, width), axis=1)
    local_sums = jnp.concatenate(
        [
            jnp.sum(v, axis=0)
            for v in (grad_gate_one, grad_mlp_in, grad_scale_two, grad_gate_two)
        ]
    )
    own_slot = (jnp.arange(tz, dtype=jnp.int32) == z).astype(f32)
    frame_sums = jnp.concatenate(
        [sum_shift_one, sum_scale_one, own_slot[:, None] * local_sums[None, :]], axis=1
    )
    share = jnp.sum(
        lax.all_to_all(
            frame_sums.reshape(tz, tz, -1).swapaxes(0, 1), "tensor", 0, 0, tiled=True
        ),
        axis=0,
    )
    shares = lax.all_gather(share, ("batch", "frames"), axis=0, tiled=True)
    grad_w_mod = mm_highest(cond_blocks.reshape(nb * blocks, width), shares)
    grad_b_mod = jnp.sum(shares, axis=0)

    grad_attn_in = collect_rows(grad_attn_part.astype(bf16), rows)
    grad_tokens = grad_mixed_one + norm_back(
        grad_attn_in * (1.0 + scale_one), normed_one, inverse_one
    )

    grad_w_arranged = mm(attn_in, grad_arranged, 0, 0)
    mine_grad = grad_w_arranged[:, : 3 * group].reshape(width, 3, 1, group)
    theirs_grad = grad_w_arranged[:, 3 * group :].reshape(width, 3, 1, group)
    grad_w_qkv = jnp.concatenate(
        [
            jnp.where(is_first, mine_grad, theirs_grad),
            jnp.where(is_first, theirs_grad, mine_grad),
        ],
        axis=2,
    ).reshape(width, 3, width_local)
    grad_w_qkv = lax.psum(grad_w_qkv.astype(bf16), ("frames", "batch")).astype(f32)
    grad_w_out = lax.all_gather(
        lax.psum_scatter(
            grad_out_weights, ("tensor", "frames", "batch"), scatter_dimension=0, tiled=True
        ),
        ("frames", "batch"),
        axis=0,
        tiled=True,
    ).astype(f32)
    grad_w_up, grad_w_down = reduce_hidden(grad_up_t, grad_down)
    return (
        result.reshape(1, 1, rows, width),
        grad_tokens.astype(bf16).reshape(1, 1, rows, width),
        grad_w_mod,
        grad_b_mod,
        grad_w_qkv,
        grad_w_out,
        grad_w_up,
        grad_w_down,
    )


def mm_highest(left, right):
    return lax.dot_general(left, right, (((0,), (0,)), ((), ())), precision=highest)


def solution(mesh):
    placed = (
        P("batch", "frames", "tensor", None),
        P("batch", "frames", "tensor", None),
        P("batch"),
        P("batch", None),
        P("batch", None),
        P(),
        P(None, "tensor"),
        P("tensor"),
        P(None, None, "tensor"),
        P("tensor", None),
        P(None, "tensor"),
        P("tensor", None),
    )
    return jax.shard_map(
        local,
        mesh=mesh,
        in_specs=placed,
        out_specs=(
            P("batch", "frames", "tensor", None),
            P("batch", "frames", "tensor", None),
            P(None, "tensor"),
            P("tensor"),
            P(None, None, "tensor"),
            P("tensor", None),
            P(None, "tensor"),
            P("tensor", None),
        ),
        check_vma=False,
    )
```
